1024 devices in a mesh: tensor: 16 (over y, x_hi, core), fsdp: 32 (over z), dp: 2 (over x_lo).
Axes of the slice: x: 4 (x_hi: 2, x_lo: 2; x = x_hi * 2 + x_lo), y: 4, z: 32, core: 2. Of those that a mesh axis runs over, the one named last changes fastest.
Arguments:
- tokens: bfloat16 [1024, 8192], P(('tensor', 'dp'), 'fsdp'), may hold values from -6 to 6
- gate_weight: bfloat16 [8192, 28672], P('fsdp', 'tensor'), may hold values from -0.0625 to 0.0625
- up_weight: bfloat16 [8192, 28672], P('fsdp', 'tensor'), may hold values from -0.0625 to 0.0625
- down_weight: bfloat16 [28672, 8192], P('tensor', 'fsdp'), may hold values from -0.03125 to 0.03125
- keep_bits: int32 [1024, 512], P(('tensor', 'dp'), 'fsdp'), may hold values from 0 to 65535
Outputs:
- mixed: bfloat16 [1024, 8192], P(('tensor', 'dp'), 'fsdp')
The draws below stay inside these ranges and needn't reach their ends.
Inputs may be any that keep to these rules, and one draw needn't show every extreme that they name: `keep_bits`: bit j of word c of a row is the keep flag of column 16 c + j of that row; every 16-bit pattern can occur.
All inputs are finite; a program needn't handle non-finite values.
Results may differ from the reference program's by a relative error of at most 0.0049.
Values may be sent and summed in bfloat16 or wider, within the bound.
A program may use at most 32 MiB of HBM per device.

```python
import jax
import jax.numpy as jnp

D = 8192
FF = 28672
TOKENS = 1024


def set_ends(values, rng, least, top_value):
    dims = values.shape
    place = [jax.random.randint(jax.random.fold_in(rng, axis), (), 0, dims[axis]) for axis in range(len(dims))]
    values = values.at[tuple(place)].set(least)
    longest = dims.index(max(dims))
    place[longest] = (place[longest] + 1) % dims[longest]
    return values.at[tuple(place)].set(top_value)


def shard_levels(key, extent, pieces, low, high):
    def one(position, shards_of):
        heights = jax.random.uniform(jax.random.fold_in(jax.random.fold_in(key, 6), position), (shards_of,), jnp.float32, low / len(pieces), high / len(pieces))
        return jnp.repeat(jnp.exp(heights), extent[position] // shards_of).reshape((-1,) + (1,) * (len(extent) - position - 1))

    gain = one(*pieces[0])
    for cut in pieces[1:]:
        gain = gain * one(*cut)
    return gain


def centred(stream_key, dims, width, most, shards=(), kind=jnp.bfloat16):
    result = width * jax.random.normal(stream_key, dims, jnp.float32)
    if shards:
        result = result * shard_levels(stream_key, dims, shards, -0.22, 0.18)
    return jnp.clip(result, -most, most).astype(kind)


def setup_inputs(seed: int = 0) -> dict:
    key_of = jax.random.split(jax.random.key(seed), 6)
    return {
        "tokens": centred(key_of[0], (TOKENS, D), 1.0, 6.0, ((0, 32), (1, 32))),
        "gate_weight": centred(key_of[1], (D, FF), D ** -0.5, 0.0625, ((0, 32), (1, 16))),
        "up_weight": centred(key_of[2], (D, FF), D ** -0.5, 0.0625, ((0, 32), (1, 16))),
        "down_weight": centred(key_of[3], (FF, D), FF ** -0.5, 0.03125, ((0, 16), (1, 32))),
        "keep_bits": set_ends(jax.random.randint(key_of[4], (TOKENS, D // 16), 0, 65536), jax.random.fold_in(key_of[4], 1), 0, 65535).astype(jnp.int32),
    }


def reference(tokens, gate_weight, up_weight, down_weight, keep_bits):
    gate = jnp.dot(tokens, gate_weight, preferred_element_type=jnp.float32)
    up = jnp.dot(tokens, up_weight, preferred_element_type=jnp.float32)
    hidden = (jax.nn.silu(gate) * up).astype(jnp.bfloat16)
    projected = jnp.dot(hidden, down_weight, preferred_element_type=jnp.float32)
    shifts = jnp.arange(16, dtype=jnp.int32)
    keep = jnp.right_shift(keep_bits[:, :, None], shifts[None, None, :]) & 1
    keep = keep.reshape(tokens.shape[0], D).astype(jnp.float32)
    return (2.0 * keep * projected).astype(jnp.bfloat16)
```

```python
import jax
import jax.numpy as jnp
from jax import lax
from jax.experimental import pallas as pl
from jax.experimental.pallas import tpu as pltpu
from jax.sharding import PartitionSpec as P

MESH = pl.DeviceIdType.MESH
BLOCK = 128
SUBS = (4, 4, 3, 3)
SCALE = 2.0**20
UNSCALE = 2.0**-20


def encode(v):
    q = v * SCALE
    q = q * jnp.abs(q)
    return (q * jnp.abs(q)).astype(jnp.bfloat16)


def decode(t):
    t = t.astype(jnp.float32)
    r = jnp.sqrt(jnp.sqrt(jnp.abs(t))) * UNSCALE
    return jnp.where(t < 0, -r, r)


def make_kernel(nt, nz, rows, depth, units, subs):
    ns = len(subs)
    offs = [sum(subs[:j]) for j in range(ns)]
    half = nz // 2
    chunk = nt * rows // nz
    per = nz // nt

    def hops(j, way):
        return half if (j % 2 == 0) == (way == 0) else half - 1

    def kernel(x_hbm, g_hbm, u_hbm, d_hbm, keep_ref, out_ref, *scratch):
        it = iter(scratch)
        xg = next(it)
        w = [next(it) for _ in range(ns)]
        wd = next(it)
        part = [next(it) for _ in range(ns)]
        rs_send = [next(it) for _ in range(ns)]
        rs_recv = [next(it) for _ in range(ns)]
        hg = [next(it) for _ in range(ns)]
        ysend, yrecv = next(it), next(it)
        x_sem, w_sem = next(it), next(it)
        xs_sem, xr_sem = next(it), next(it)
        rss_sem, rsr_sem = next(it), next(it)
        ags_sem, agr_sem = next(it), next(it)
        ys_sem, yr_sem = next(it), next(it)

        t = lax.axis_index("tensor")
        z = lax.axis_index("fsdp")
        ring = (lax.rem(z + 1, nz), lax.rem(z + nz - 1, nz))
        sign = (1, -1)

        def peer(o):
            return lax.rem(t + o, nt)

        x_copy = pltpu.make_async_copy(x_hbm, xg.at[0], x_sem)
        x_copy.start()
        w_copies = []
        for j in range(ns):
            cols = pl.ds(offs[j], subs[j])
            pair = (
                pltpu.make_async_copy(g_hbm.at[:, cols], w[j].at[:, : subs[j]], w_sem.at[2 * j]),
                pltpu.make_async_copy(u_hbm.at[:, cols], w[j].at[:, subs[j] :], w_sem.at[2 * j + 1]),
            )
            for c in pair:
                c.start()
            w_copies.append(pair)
        d_copy = pltpu.make_async_copy(d_hbm, wd, w_sem.at[2 * ns])
        d_copy.start()

        barrier = pltpu.get_barrier_semaphore()
        for way in range(2):
            pl.semaphore_signal(barrier, inc=1, device_id={"fsdp": ring[way]}, device_id_type=MESH)
        for o in range(1, nt):
            pl.semaphore_signal(barrier, inc=1, device_id={"tensor": peer(o)}, device_id_type=MESH)
        pl.semaphore_wait(barrier, nt + 1)

        x_copy.wait()

        def x_send(o):
            return pltpu.make_async_remote_copy(
                src_ref=xg.at[0],
                dst_ref=xg.at[nt - o],
                send_sem=xs_sem.at[o],
                recv_sem=xr_sem.at[nt - o],
                device_id={"tensor": peer(o)},
                device_id_type=MESH,
            )

        for o in range(1, nt):
            x_send(o).start()
        for o in range(1, nt):
            x_send(nt - o).wait_recv()

        def rs_copy(s, j, way):
            return pltpu.make_async_remote_copy(
                src_ref=rs_send[j].at[way, s],
                dst_ref=rs_recv[j].at[way, s],
                send_sem=rss_sem.at[way, s, j],
                recv_sem=rsr_sem.at[way, s, j],
                device_id={"fsdp": ring[way]},
                device_id_type=MESH,
            )

        def dest(s, j, way):
            return lax.rem(z + sign[way] * (hops(j, way) - s) + nz, nz)

        def rs_step(s, j, way):
            v = part[j][dest(s, j, way)]
            if not (isinstance(s, int) and s == 0):
                rs_copy(s - 1, j, way).wait_recv()
                v = v + decode(rs_recv[j][way, s - 1])
            rs_send[j][way, s] = encode(v)
            rs_copy(s, j, way).start()

        tile_rows = 256
        for j in range(ns):
            for c in w_copies[j]:
                c.wait()
            tile_cols = 2 * BLOCK

            def tile(r, _, j=j):
                xb = xg[pl.ds(r * (tile_rows // rows), tile_rows // rows)].reshape(tile_rows, depth)
                for c in range(2 * subs[j] // tile_cols):
                    cols = pl.ds(c * tile_cols, tile_cols)
                    p = jnp.dot(xb, w[j][:, cols], preferred_element_type=jnp.float32)
                    part[j][pl.ds(r * (tile_rows // chunk), tile_rows // chunk), :, cols] = p.reshape(
                        tile_rows // chunk, chunk, tile_cols
                    )
                return 0

            lax.fori_loop(0, nt * rows // tile_rows, tile, 0)
            for way in range(2):
                rs_step(0, j, way)

        def rs_loop(s, _):
            for j in range(ns):
                for way in range(2):
                    rs_step(s, j, way)
            return 0

        lax.fori_loop(1, half - 1, rs_loop, 0)
        for j in range(ns):
            for way in range(2):
                if hops(j, way) == half:
                    rs_step(half - 1, j, way)

        def ag_copy(s, j, way):
            b = lax.rem(z - sign[way] * s + nz, nz)
            return pltpu.make_async_remote_copy(
                src_ref=hg[j].at[b],
                dst_ref=hg[j].at[b],
                send_sem=ags_sem.at[way, s, j],
                recv_sem=agr_sem.at[way, s, j],
                device_id={"fsdp": ring[way]},
                device_id_type=MESH,
            )

        def ag_wait(s, j, way):
            b = lax.rem(z - sign[way] * (s + 1) + nz, nz)
            pltpu.make_async_remote_copy(
                src_ref=hg[j].at[b],
                dst_ref=hg[j].at[b],
                send_sem=ags_sem.at[way, s, j],
                recv_sem=agr_sem.at[way, s, j],
                device_id={"fsdp": ring[way]},
                device_id_type=MESH,
            ).wait_recv()

        for j in range(ns):
            v = part[j][z]
            for way in range(2):
                last = hops(j, way) - 1
                rs_copy(last, j, way).wait_recv()
                v = v + decode(rs_recv[j][way, last])
            gate, up = v[:, : subs[j]], v[:, subs[j] :]
            hg[j][z] = (gate / (1.0 + jnp.exp(-gate)) * up).astype(jnp.bfloat16)
            for way in range(2):
                ag_copy(0, j, way).start()

        d_copy.wait()

        width = out_ref.shape[1]
        words = keep_ref[...]
        nw = words.shape[1]
        hot = (
            lax.broadcasted_iota(jnp.int32, (nw, width), 1) // 16 == lax.broadcasted_iota(jnp.int32, (nw, width), 0)
        ).astype(jnp.bfloat16)
        low = jnp.dot((words & 255).astype(jnp.bfloat16), hot, preferred_element_type=jnp.float32)
        high = jnp.dot((words >> 8).astype(jnp.bfloat16), hot, preferred_element_type=jnp.float32)
        bit = lax.broadcasted_iota(jnp.int32, (rows, width), 1) % 16
        word = low.astype(jnp.int32) + (high.astype(jnp.int32) << 8)
        keep2 = 2.0 * ((word >> bit) & 1).astype(jnp.float32)

        odd = lax.rem(z, 2)
        turn = 1 - 2 * odd
        mid = z // 2

        def y_copy(q):
            return pltpu.make_async_remote_copy(
                src_ref=ysend.at[q],
                dst_ref=yrecv.at[q],
                send_sem=ys_sem.at[q],
                recv_sem=yr_sem.at[q],
                device_id={"tensor": peer(q)},
                device_id_type=MESH,
            )

        def down(k):
            m = k // 2
            q = lax.rem(mid + turn * m * (2 * lax.rem(k, 2) - 1) + nt, nt)
            y = jnp.zeros((rows, width), jnp.float32)
            for j in range(ns):
                h = hg[j][pl.ds(q * per, per)].reshape(rows, subs[j])
                y = y + jnp.dot(h, wd[pl.ds(offs[j], subs[j]), :], preferred_element_type=jnp.float32)

            @pl.when(q == 0)
            def _():
                yrecv[0] = y

            @pl.when(q != 0)
            def _():
                ysend[q] = y
                y_copy(q).start()

        def ag_loop(k, _):
            for j in range(ns):
                for way in range(2):
                    ag_wait(k - 1, j, way)
                    ag_copy(k, j, way).start()
            down(k)
            return 0

        lax.fori_loop(1, half - 1, ag_loop, 0)
        for j in range(ns):
            for way in range(2):
                ag_wait(half - 2, j, way)
                if hops(j, way) == half:
                    ag_copy(half - 1, j, way).start()
        down(half - 1)
        for j in range(ns):
            for way in range(2):
                if hops(j, way) == half:
                    ag_wait(half - 1, j, way)
        down(half)

        for o in range(1, nt):
            x_send(o).wait_send()

        def drain(s, _):
            for j in range(ns):
                for way in range(2):
                    rs_copy(s, j, way).wait_send()
                    ag_copy(s, j, way).wait_send()
            return 0

        lax.fori_loop(0, half - 1, drain, 0)
        for j in range(ns):
            for way in range(2):
                if hops(j, way) == half:
                    rs_copy(half - 1, j, way).wait_send()
                    ag_copy(half - 1, j, way).wait_send()

        total = yrecv[0]
        for q in range(1, nt):
            y_copy(q).wait_recv()
            total = total + yrecv[q]
        out_ref[...] = (keep2 * total).astype(out_ref.dtype)
        for q in range(1, nt):
            y_copy(q).wait_send()

    return kernel


def solution(mesh):
    nt, nz = mesh.shape["tensor"], mesh.shape["fsdp"]

    def step(tokens, gate_weight, up_weight, down_weight, keep_bits):
        rows, depth = tokens.shape
        units = gate_weight.shape[1]
        width = down_weight.shape[1]
        subs = [b * BLOCK for b in SUBS]
        assert sum(subs) == units
        ns = len(subs)
        half, chunk = nz // 2, nt * rows // nz
        bf, f32 = jnp.bfloat16, jnp.float32
        dma = pltpu.SemaphoreType.DMA
        hbm = pl.BlockSpec(memory_space=pl.ANY)
        vmem = pl.BlockSpec(memory_space=pltpu.VMEM)
        return pl.pallas_call(
            make_kernel(nt, nz, rows, depth, units, subs),
            out_shape=jax.ShapeDtypeStruct((rows, width), bf),
            in_specs=[hbm, hbm, hbm, hbm, vmem],
            out_specs=vmem,
            scratch_shapes=[
                pltpu.VMEM((nt, rows, depth), bf),
                *[pltpu.VMEM((depth, 2 * n), bf) for n in subs],
                pltpu.VMEM((units, width), bf),
                *[pltpu.VMEM((nz, chunk, 2 * n), f32) for n in subs],
                *[pltpu.VMEM((2, half, chunk, 2 * n), bf) for n in subs],
                *[pltpu.VMEM((2, half, chunk, 2 * n), bf) for n in subs],
                *[pltpu.VMEM((nz, chunk, n), bf) for n in subs],
                pltpu.VMEM((nt, rows, width), f32),
                pltpu.VMEM((nt, rows, width), f32),
                dma,
                dma((2 * ns + 1,)),
                dma((nt,)),
                dma((nt,)),
                dma((2, half, ns)),
                dma((2, half, ns)),
                dma((2, half, ns)),
                dma((2, half, ns)),
                dma((nt,)),
                dma((nt,)),
            ],
            compiler_params=pltpu.CompilerParams(
                collective_id=0, has_side_effects=True, vmem_limit_bytes=48 * 1024 * 1024
            ),
            name="ffn",
        )(tokens, gate_weight, up_weight, down_weight, keep_bits)

    return jax.shard_map(
        step,
        mesh=mesh,
        in_specs=(
            P(("tensor", "dp"), "fsdp"),
            P("fsdp", "tensor"),
            P("fsdp", "tensor"),
            P("tensor", "fsdp"),
            P(("tensor", "dp"), "fsdp"),
        ),
        out_specs=P(("tensor", "dp"), "fsdp"),
        check_vma=False,
    )
```
